32 devices in a mesh: context: 16 (over z, x, core), tensor: 2 (over y).
Axes of the slice: x: 2, y: 2, z: 4, core: 2. Of those that a mesh axis runs over, the one named last changes fastest.
Arguments:
- head_inputs: bfloat16 [2048, 8192], P('context', 'tensor'), may hold values from -6 to 6
- step_sizes: float32 [128, 2048], P('tensor', 'context'), may hold values from 0.5 to 1.5
- decay_rate: float32 [128], P('tensor'), may hold values from 0.000146484375 to 0.05
- input_map: bfloat16 [2048, 1024], P('context', 'tensor'), may hold values from -0.5 to 0.5
- output_map: bfloat16 [2048, 1024], P('context', 'tensor'), may hold values from -0.5 to 0.5
- document: int32 [2048], P('context'), may hold values from 0 to 2, never falling along the last dimension, each value on 1 to 1024 neighbouring positions
- grad_output: bfloat16 [2048, 8192], P(('context', 'tensor')), may hold values from -6 to 6
Outputs:
- grad_inputs: bfloat16 [2048, 8192], P('context', 'tensor')
- grad_steps: float32 [128, 2048], P('tensor', 'context')
- grad_in_map: float32 [2048, 1024], P('context', 'tensor')
- grad_out_map: float32 [2048, 1024], P('context', 'tensor')
The draws below stay inside these ranges and needn't reach their ends.
Inputs may be any that keep to these rules, and one draw needn't show every extreme that they name: document numbers never fall along the tokens; each document has 1 to 1024 tokens, one exactly 1024.
All inputs are finite; a program needn't handle non-finite values.
Results may differ from the reference program's by a relative error of at most 0.001.
Values may be sent and summed in bfloat16 or wider, within the bound.
A program may use at most 192 MiB of HBM per device.

```python
import math
import jax
import jax.numpy as jnp
import numpy as np
from jax import lax

H = 128
P_SIZE = 64
N = 128
G = 8
BLOCK = 128
DOCS = 3
TOKENS = 2048
DOC_MOST = 1024


def draw_decay_rate(key, part):
    folded = jax.random.fold_in(key, 101)
    key_coin, key_slow, key_fast = jax.random.split(folded, 3)
    share = 0.5
    coin = jax.random.uniform(key_coin, (H,), jnp.float32) < share
    slow = jnp.exp(jax.random.uniform(key_slow, (H,), jnp.float32, minval=math.log(0.3 / TOKENS), maxval=math.log(2.0 / TOKENS)))
    fast = jnp.exp(jax.random.uniform(key_fast, (H,), jnp.float32, minval=math.log(1.0 / 50.0), maxval=math.log(1.0 / 20.0)))
    return jnp.where(coin, slow, fast).astype(jnp.float32)


def draw_step_sizes(key, part):
    folded = jax.random.fold_in(key, 202)
    level = jax.random.uniform(folded, (H, TOKENS), jnp.float32)
    values = 0.5 + level
    return values.astype(jnp.float32)


def block_scale(stream_key, shape, pieces, smallest, high):
    loudness = 1.0
    for axis_at, shards_of in pieces:
        steps = jax.random.uniform(jax.random.fold_in(jax.random.fold_in(stream_key, 6), axis_at), (shards_of,), jnp.float32, smallest / len(pieces), high / len(pieces))
        loudness = loudness * jnp.repeat(jnp.exp(steps), shape[axis_at] // shards_of).reshape((-1,) + (1,) * (len(shape) - 1 - axis_at))
    return loudness


def split_up(count, total, limit, skew):
    portions = [(1 << 20) // math.isqrt(rank ** skew) + 1 for rank in range(2, count + 1)]
    rest, holding = total - limit - (count - 1), [1] * (count - 1)
    while rest > 0:
        free = [i for i in range(count - 1) if holding[i] < limit]
        mass, budget = sum([portions[i] for i in free]), rest
        for i in free:
            more = min(limit - holding[i], max(1, budget * portions[i] // mass), rest)
            holding[i] = holding[i] + more
            rest = rest - more
    return np.array([limit] + holding)


def ragged_sizes(stream_key, amount, total, bound, skew):
    if amount == 2:
        one = jax.random.randint(stream_key, (), max(1, total - bound), min(bound, total - 1) + 1)
        return jnp.stack([one, total - one])
    sizes = jnp.asarray(split_up(amount, total, bound, skew), jnp.int32)
    pairs = (amount - 1) // 2
    donor, receiver = sizes[1:1 + 2 * pairs:2], sizes[2:2 + 2 * pairs:2]
    room = jnp.minimum(donor - 1, bound - receiver)
    shifted = jax.random.randint(jax.random.fold_in(stream_key, 1), (pairs,), 0, 1 << 20) % (room + 1)
    sizes = sizes.at[1:1 + 2 * pairs:2].set(donor - shifted).at[2:2 + 2 * pairs:2].set(receiver + shifted)
    return sizes[jax.random.permutation(jax.random.fold_in(stream_key, 2), amount)]


def gaussian(rng, extent, deviation, limit, shards=(), dtype=jnp.bfloat16):
    entries = jax.random.normal(rng, extent, jnp.float32) * deviation
    if len(shards) > 0:
        entries = block_scale(rng, extent, shards, -0.22, 0.18) * entries
    return jnp.clip(entries, min=-limit, max=limit).astype(dtype)


def setup_inputs(seed: int = 0) -> dict:
    key_list = jax.random.split(jax.random.key(seed), 8)
    return {
        "head_inputs": gaussian(key_list[0], (TOKENS, H * P_SIZE), 1.0, 6.0, ((0, 16), (1, 2))),
        "step_sizes": draw_step_sizes(jax.random.fold_in(key_list[7], 71), 0),
        "decay_rate": draw_decay_rate(jax.random.fold_in(key_list[7], 71), 0),
        "input_map": gaussian(key_list[3], (TOKENS, G * N), N ** -0.5, 0.5, ((0, 16), (1, 2))),
        "output_map": gaussian(key_list[4], (TOKENS, G * N), N ** -0.5, 0.5, ((0, 16), (1, 2))),
        "document": jnp.searchsorted(jnp.cumsum(ragged_sizes(key_list[5], DOCS, TOKENS, DOC_MOST, 0)), jnp.arange(TOKENS), side="right").astype(jnp.int32),
        "grad_output": gaussian(key_list[6], (TOKENS, H * P_SIZE), 1.0, 6.0, ((0, 32),)),
    }


HIGH = lax.Precision.HIGHEST


def block_terms(steps_block, ids_block, prev_id, next_id, rates_grouped):
    length = ids_block.shape[0]
    positions = jnp.arange(length)
    same_doc = (ids_block[:, None] == ids_block[None, :]) & (positions[:, None] >= positions[None, :])
    cumul = jnp.cumsum(-rates_grouped[..., None] * steps_block, axis=-1)
    differ = cumul[..., :, None] - cumul[..., None, :]
    weights = jnp.where(same_doc, jnp.exp(jnp.where(same_doc, differ, 0.0)), 0.0)
    last_sum = cumul[..., -1:]
    in_coef = jnp.exp(cumul) * (ids_block == prev_id).astype(jnp.float32)
    out_coef = jnp.exp(last_sum - cumul) * (ids_block == next_id).astype(jnp.float32)
    end_coef = jnp.exp(last_sum - cumul) * (ids_block == ids_block[-1]).astype(jnp.float32)
    linked = (ids_block[-1] == prev_id).astype(jnp.float32)
    decay_all = jnp.exp(last_sum[..., 0]) * linked
    return same_doc, weights, in_coef, out_coef, end_coef, linked, decay_all


def reference(head_inputs, step_sizes, decay_rate, input_map, output_map, document, grad_output):
    blocks = TOKENS // BLOCK
    per_group = H // G
    inputs_b = head_inputs.reshape(blocks, BLOCK, G, per_group, P_SIZE)
    grads_b = grad_output.reshape(blocks, BLOCK, G, per_group, P_SIZE)
    steps_b = jnp.transpose(step_sizes.reshape(G, per_group, blocks, BLOCK), (2, 0, 1, 3))
    rates_grouped = decay_rate.reshape(G, per_group)
    in_b = input_map.reshape(blocks, BLOCK, G, N)
    out_b = output_map.reshape(blocks, BLOCK, G, N)
    ids_b = document.reshape(blocks, BLOCK).astype(jnp.int32)
    missing = jnp.full((1,), -1, jnp.int32)
    prev_ids = jnp.concatenate([missing, ids_b[:-1, -1]]).astype(jnp.int32)
    next_ids = jnp.concatenate([ids_b[1:, 0], missing]).astype(jnp.int32)
    stacked = (inputs_b, grads_b, steps_b, in_b, out_b, ids_b, prev_ids, next_ids)

    def prepare(item):
        inputs_k, grads_k, steps_k, in_k, out_k, ids_k, prev_id, next_id = item
        terms = block_terms(steps_k, ids_k, prev_id, next_id, rates_grouped)
        scaled = inputs_k.astype(jnp.float32) * jnp.moveaxis(steps_k, -1, 0)[..., None]
        in_f = in_k.astype(jnp.float32)
        out_f = out_k.astype(jnp.float32)
        grads_f = grads_k.astype(jnp.float32)
        cross = jnp.einsum('ign,jgn->gij', out_f, in_f, precision=HIGH)
        mixing = terms[1] * cross[:, None]
        return terms, scaled, in_f, out_f, grads_f, mixing

    def forward(state, item):
        terms, scaled, in_f, out_f, grads_f, mixing = prepare(item)
        same_doc, weights, in_coef, out_coef, end_coef, linked, decay_all = terms
        outputs = jnp.einsum('ghij,jghp->ighp', mixing, scaled, precision=HIGH)
        outputs = outputs + jnp.einsum('ign,ghnp,ghi->ighp', out_f, state, in_coef, precision=HIGH)
        agree = jnp.sum(grads_f * outputs, axis=-1)
        carried = jnp.einsum('ighp,ghnp,ghi->ign', grads_f, state, in_coef, precision=HIGH)
        fresh = jnp.einsum('jgn,ghj,jghp->ghnp', in_f, end_coef, scaled, precision=HIGH)
        state = decay_all[..., None, None] * state + fresh
        return state, (agree, carried)

    zero_state = jnp.zeros((G, per_group, N, P_SIZE), jnp.float32)
    zero_tail = jnp.zeros((G, per_group), jnp.float32)
    _, (agree_all, carried_all) = lax.scan(forward, zero_state, stacked)

    def backward(carry, item_all):
        adjoint, tail = carry
        item, agree, carried = item_all
        terms, scaled, in_f, out_f, grads_f, mixing = prepare(item)
        same_doc, weights, in_coef, out_coef, end_coef, linked, decay_all = terms
        ids_k, prev_id, next_id = item[5], item[6], item[7]
        update = jnp.einsum('ghij,ighp->jghp', mixing, grads_f, precision=HIGH)
        update = update + jnp.einsum('jgn,ghnp,ghj->jghp', in_f, adjoint, out_coef, precision=HIGH)
        inputs_f = item[0].astype(jnp.float32)
        steps_rows = jnp.moveaxis(item[2], -1, 0)
        grad_in = (update * steps_rows[..., None]).astype(jnp.bfloat16)
        step_part = jnp.sum(inputs_f * update, axis=-1)
        slope = agree - jnp.sum(scaled * update, axis=-1)
        slope_heads = jnp.moveaxis(slope, 0, -1)
        tails = jnp.einsum('ghi,ij->ghj', slope_heads, same_doc.astype(jnp.float32), precision=HIGH)
        tails = tails + tail[..., None] * (ids_k == next_id).astype(jnp.float32)
        grad_steps = jnp.moveaxis(step_part, 0, -1) - rates_grouped[..., None] * tails
        products = jnp.einsum('ighp,jghp->ghij', grads_f, scaled, precision=HIGH)
        score_grad = jnp.sum(weights * products, axis=1)
        grad_c = jnp.einsum('gij,jgn->ign', score_grad, in_f, precision=HIGH) + carried
        grad_b = jnp.einsum('gij,ign->jgn', score_grad, out_f, precision=HIGH)
        grad_b = grad_b + jnp.einsum('jghp,ghnp,ghj->jgn', scaled, adjoint, out_coef, precision=HIGH)
        message = jnp.einsum('ign,ghi,ighp->ghnp', out_f, in_coef, grads_f, precision=HIGH)
        adjoint = decay_all[..., None, None] * adjoint + message
        tail = linked * tail + jnp.sum(slope_heads * (ids_k == prev_id).astype(jnp.float32), axis=-1)
        return (adjoint, tail), (grad_in, grad_steps, grad_b, grad_c)

    _, (grad_in_all, grad_steps_all, grad_b_all, grad_c_all) = lax.scan(
        backward, (zero_state, zero_tail), (stacked, agree_all, carried_all), reverse=True)
    grad_inputs = grad_in_all.reshape(TOKENS, H * P_SIZE)
    grad_steps = jnp.transpose(grad_steps_all, (1, 2, 0, 3)).reshape(H, TOKENS)
    grad_in_map = grad_b_all.reshape(TOKENS, G * N)
    grad_out_map = grad_c_all.reshape(TOKENS, G * N)
    return grad_inputs, grad_steps, grad_in_map, grad_out_map
```

```python
import functools

import jax
import jax.numpy as jnp
from jax import lax
from jax.experimental import pallas as pl
from jax.experimental.pallas import tpu as pltpu
from jax.sharding import PartitionSpec as P

H = 128
P_SIZE = 64
N = 128
G = 8
SPAN = 128
PER = H // G
WIDE = PER * P_SIZE
LANES = 128
MESH = pl.DeviceIdType.MESH
BF = jnp.bfloat16
F32 = jnp.float32
NN = (((1,), (0,)), ((), ()))
NT = (((1,), (1,)), ((), ()))
TN = (((0,), (0,)), ((), ()))


def split(a):
    hi = a.astype(BF)
    return hi, (a - hi.astype(F32)).astype(BF)


def mm(a, b, dims=NN):
    return lax.dot_general(a, b, dims, preferred_element_type=F32)


def left2(a, b, dims=NN):
    hi, lo = split(a)
    return mm(hi, b, dims) + mm(lo, b, dims)


def right2(a, b, dims=NN):
    hi, lo = split(b)
    return mm(a, hi, dims) + mm(a, lo, dims)


def both3(a, b, dims=NN):
    ah, al = split(a)
    bh, bl = split(b)
    return mm(ah, bh, dims) + mm(ah, bl, dims) + mm(al, bh, dims)


def spreader():
    row = lax.broadcasted_iota(jnp.int32, (LANES, WIDE), 0)
    col = lax.broadcasted_iota(jnp.int32, (LANES, WIDE), 1)
    return jnp.where(row == col // P_SIZE, 1.0, 0.0).astype(BF)


def rows(k, size=SPAN):
    return pl.ds(k * size, size)


def ids_of(ranks):
    context = lax.axis_index("context")
    tensor = lax.axis_index("tensor")
    rank = lax.rem(context, ranks)
    return context - rank, rank, tensor


def greet(ranks, tensors, base, rank, tensor):
    barrier = pltpu.get_barrier_semaphore()
    for dr in range(ranks):
        for dt in range(tensors):
            if dr or dt:
                peer = {
                    "context": base + lax.rem(rank + dr, ranks),
                    "tensor": lax.rem(tensor + dt, tensors) if tensors > 1 else tensor,
                }
                pl.semaphore_signal(barrier, inc=1, device_id=peer, device_id_type=MESH)
    if ranks * tensors > 1:
        pl.semaphore_wait(barrier, ranks * tensors - 1)


def gather_kernel(ranks, tensors, x, b, c, dt, dy, xg, bg, cg, dtg, dyg, send, recv, local):
    base, rank, tensor = ids_of(ranks)
    greet(ranks, tensors, base, rank, tensor)
    part = dy.shape[0]
    spot = pl.multiple_of(rank * SPAN, SPAN)
    spot_dy = pl.multiple_of((rank * tensors + tensor) * part, part)
    copies = []
    order = [r for r in range(ranks) if r % 2 == 0] + [r for r in range(ranks) if r % 2]
    for dr in order[1:] + order[:1]:
        to = lax.rem(rank + dr, ranks)
        pairs = [
            (x.at[:, pl.ds(pl.multiple_of(to * WIDE, WIDE), WIDE)], xg.at[pl.ds(spot, SPAN), :]),
            (b.at[:, pl.ds(pl.multiple_of(to * N, N), N)], bg.at[pl.ds(spot, SPAN), :]),
            (c.at[:, pl.ds(pl.multiple_of(to * N, N), N)], cg.at[pl.ds(spot, SPAN), :]),
            (dt.at[pl.ds(pl.multiple_of(to * PER, PER), PER), :], dtg.at[rank]),
        ]
        for n, (src, dst) in enumerate(pairs):
            if dr == 0:
                copy = pltpu.make_async_copy(src, dst, local.at[n])
            else:
                copy = pltpu.make_async_remote_copy(
                    src_ref=src,
                    dst_ref=dst,
                    send_sem=send.at[dr * 4 + n],
                    recv_sem=recv.at[dr * 4 + n],
                    device_id={"context": base + to, "tensor": tensor},
                    device_id_type=MESH,
                )
            copy.start()
            copies.append(copy)
        for du in range(tensors):
            tt = lax.rem(tensor + du, tensors)
            at = pl.multiple_of((tt * ranks + to) * WIDE, WIDE)
            src, dst = dy.at[:, pl.ds(at, WIDE)], dyg.at[pl.ds(spot_dy, part), :]
            if dr == 0 and du == 0:
                copy = pltpu.make_async_copy(src, dst, local.at[4])
            else:
                n = ranks * 4 + dr * tensors + du
                copy = pltpu.make_async_remote_copy(
                    src_ref=src,
                    dst_ref=dst,
                    send_sem=send.at[n],
                    recv_sem=recv.at[n],
                    device_id={"context": base + to, "tensor": tt},
                    device_id_type=MESH,
                )
            copy.start()
            copies.append(copy)
    for copy in copies:
        copy.wait()


def scatter_kernel(ranks, gi, gs, gb, gc, gi_o, gs_o, gb_o, gc_o, send, recv, local):
    base, rank, tensor = ids_of(ranks)
    greet(ranks, 1, base, rank, tensor)
    wide_at = pl.multiple_of(rank * WIDE, WIDE)
    map_at = pl.multiple_of(rank * N, N)
    head_at = pl.multiple_of(rank * PER, PER)
    copies = []
    order = [r for r in range(ranks) if r % 2 == 0] + [r for r in range(ranks) if r % 2]
    for dr in order[1:] + order[:1]:
        to = lax.rem(rank + dr, ranks)
        spot = pl.multiple_of(to * SPAN, SPAN)
        pairs = [
            (gi.at[pl.ds(spot, SPAN), :], gi_o.at[:, pl.ds(wide_at, WIDE)]),
            (gb.at[pl.ds(spot, SPAN), :], gb_o.at[:, pl.ds(map_at, N)]),
            (gc.at[pl.ds(spot, SPAN), :], gc_o.at[:, pl.ds(map_at, N)]),
            (gs.at[to], gs_o.at[pl.ds(head_at, PER), :]),
        ]
        for n, (src, dst) in enumerate(pairs):
            if dr == 0:
                copy = pltpu.make_async_copy(src, dst, local.at[n])
            else:
                copy = pltpu.make_async_remote_copy(
                    src_ref=src,
                    dst_ref=dst,
                    send_sem=send.at[dr * 4 + n],
                    recv_sem=recv.at[dr * 4 + n],
                    device_id={"context": base + to, "tensor": tensor},
                    device_id_type=MESH,
                )
            copy.start()
            copies.append(copy)
    for copy in copies:
        copy.wait()


def summary_kernel(
    ranks, x, b, c, dt, dy, rate, tok, fresh, message, ltok, lhead, dttok, f_out, m_out, d_out
):
    spread = spreader()
    up = (
        lax.broadcasted_iota(jnp.int32, (SPAN, SPAN), 0)
        <= lax.broadcasted_iota(jnp.int32, (SPAN, SPAN), 1)
    ).astype(F32)
    pad = jnp.zeros((LANES - PER, SPAN), F32)
    decays = []
    for k in range(ranks):
        steps = dt[k]
        cum = lax.dot_general(
            -rate[...] * steps, up, NN, precision=lax.Precision.HIGHEST, preferred_element_type=F32
        )
        lhead[k] = cum
        cum_t = jnp.transpose(jnp.concatenate([cum, pad], axis=0))
        dt_t = jnp.transpose(jnp.concatenate([steps, pad], axis=0))
        ltok[rows(k), :] = cum_t
        dttok[rows(k), :] = dt_t
        mask_in = tok[rows(k), 1:2]
        mask_end = tok[rows(k), 3:4]
        in_coef = jnp.exp(cum_t) * mask_in
        end_coef = jnp.exp(cum_t[SPAN - 1 :, :] - cum_t) * mask_end * dt_t
        xs = x[rows(k), :].astype(F32) * left2(end_coef, spread)
        in_e = left2(in_coef, spread)
        dyc = dy[rows(k), :].astype(F32) * in_e
        fresh[k] = right2(b[rows(k), :], xs, TN)
        message[k] = right2(c[rows(k), :], dyc, TN)
        decays.append(in_e[SPAN - 1 :, :])
    total = fresh[0]
    decay = decays[0]
    for k in range(1, ranks):
        total = decays[k] * total + fresh[k]
        decay = decay * decays[k]
    f_out[...] = total
    d_out[...] = decay
    back = message[ranks - 1]
    for k in range(ranks - 2, -1, -1):
        back = decays[k] * back + message[k]
    m_out[...] = back


def local_kernel(x, b, c, dy, ltok, lhead, dttok, tok, idrow, u, agree, gb, gc):
    cross_t = mm(b[...], c[...], NT)
    later = lax.broadcasted_iota(jnp.int32, (SPAN, SPAN), 1) >= lax.broadcasted_iota(
        jnp.int32, (SPAN, SPAN), 0
    )
    same = tok[:, 0:1] == idrow[...]
    neg = jnp.where(later & same, 0.0, -1e30)
    score = jnp.zeros((SPAN, SPAN), F32)
    for h in range(PER):
        cut = slice(h * P_SIZE, (h + 1) * P_SIZE)
        x_h = x[:, cut]
        dy_h = dy[:, cut]
        w = jnp.exp((lhead[0, h : h + 1, :] - ltok[:, h : h + 1]) + neg)
        u[:, cut] = left2(w * cross_t, dy_h)
        q = w * mm(x_h, dy_h, NT) * dttok[:, h : h + 1]
        score = score + q
        agree[0, h : h + 1, :] = jnp.sum(q * cross_t, axis=0, keepdims=True)
    gb[...] = left2(score, c[...])
    gc[...] = left2(score, b[...], TN)


def finish_kernel(
    ranks, x, b, c, dy, rate, tok, idrow, ltok, dttok, u, agree, gb_l, gc_l, fresh, message,
    s_in, a_in, gi, gs, gb, gc, states,
):
    spread = spreader()
    states[0] = s_in[...]
    for k in range(ranks):
        last = ltok[k * SPAN + SPAN - 1 : k * SPAN + SPAN, :]
        link = tok[k * SPAN + SPAN - 1 : k * SPAN + SPAN, 1:2]
        decay = left2(jnp.broadcast_to(jnp.exp(last) * link, (8, LANES)), spread)[:1]
        states[k + 1] = decay * states[k] + fresh[k]
    pad = jnp.zeros((LANES - PER, SPAN), F32)
    earlier = lax.broadcasted_iota(jnp.int32, (SPAN, SPAN), 0) <= lax.broadcasted_iota(
        jnp.int32, (SPAN, SPAN), 1
    )
    rate_row = jnp.transpose(
        jnp.concatenate([jnp.broadcast_to(rate[...], (PER, SPAN)), pad], axis=0)
    )
    adj = a_in[...]
    for k in range(ranks - 1, -1, -1):
        at = rows(k)
        cum = ltok[at, :]
        dt_t = dttok[at, :]
        mask_in = tok[at, 1:2]
        mask_out = tok[at, 2:3]
        in_coef = jnp.exp(cum) * mask_in
        out_coef = jnp.exp(cum[SPAN - 1 :, :] - cum) * mask_out
        in_e = left2(in_coef, spread)
        out_e = left2(out_coef, spread)
        dt_e = left2(dt_t, spread)
        state = states[k]
        x_f = x[at, :].astype(F32)
        dyc = dy[at, :].astype(F32) * in_e
        total_u = u[at, :] + right2(b[at, :], adj) * out_e
        gi[at, :] = (total_u * dt_e).astype(BF)
        gc[at, :] = gc_l[at, :] + both3(dyc, state, NT)
        gb[at, :] = gb_l[at, :] + both3(x_f * out_e * dt_e, adj, NT)
        agree_t = jnp.transpose(jnp.concatenate([agree[k], pad], axis=0))
        dy_y = agree_t + left2(dyc * right2(c[at, :], state), spread, NT)
        xu = left2(x_f * total_u, spread, NT)
        slope = dy_y - dt_t * xu
        same = (tok[at, 0:1] == idrow[:, at]) & earlier
        meet = jnp.sum(states[k + 1] * adj, axis=0, keepdims=True)
        tail_carry = left2(jnp.broadcast_to(meet, (8, WIDE)), spread, NT)[:1]
        tails = right2(jnp.where(same, 1.0, 0.0).astype(BF), slope) + tail_carry * mask_out
        gs[k] = jnp.transpose(xu - rate_row * tails)[:PER, :]
        adj = in_e[SPAN - 1 :, :] * adj + message[k]


def shards(head_inputs, step_sizes, decay_rate, input_map, output_map, document, grad_output):
    heads_here = decay_rate.shape[0]
    ranks = heads_here // PER
    contexts = lax.axis_size("context")
    tensors = lax.axis_size("tensor")
    planes = contexts // ranks
    tokens = ranks * SPAN
    context = lax.axis_index("context")
    rank = context % ranks
    anywhere = pl.BlockSpec(memory_space=pl.ANY)
    vmem = pl.BlockSpec(memory_space=pltpu.VMEM)
    shape = jax.ShapeDtypeStruct

    ids = lax.all_gather(document, "context", tiled=True).astype(F32)
    blocks = ids.reshape(contexts, SPAN)
    none = jnp.full((1,), -1.0, F32)
    prev = jnp.concatenate([none, blocks[:-1, -1]])
    after = jnp.concatenate([blocks[1:, 0], none])
    marks = jnp.stack(
        [
            blocks,
            (blocks == prev[:, None]).astype(F32),
            (blocks == after[:, None]).astype(F32),
            (blocks == blocks[:, -1:]).astype(F32),
        ],
        axis=-1,
    ).reshape(contexts * SPAN, 4)
    start = (context - rank) * SPAN
    tok = lax.dynamic_slice(marks, (start, 0), (tokens, 4))
    idrow = lax.dynamic_slice(ids, (start,), (tokens,))[None, :]
    rate = lax.dynamic_slice(decay_rate, (rank * PER,), (PER,))[:, None]

    n_in = ranks * 4 + ranks * tensors
    xg, bg, cg, dtg, dyg = pl.pallas_call(
        functools.partial(gather_kernel, ranks, tensors),
        out_shape=(
            shape((tokens, WIDE), BF),
            shape((tokens, N), BF),
            shape((tokens, N), BF),
            shape((ranks, PER, SPAN), F32),
            shape((tokens, WIDE), BF),
        ),
        in_specs=[anywhere] * 5,
        out_specs=(anywhere,) * 5,
        scratch_shapes=[
            pltpu.SemaphoreType.DMA((n_in,)),
            pltpu.SemaphoreType.DMA((n_in,)),
            pltpu.SemaphoreType.DMA((5,)),
        ],
        compiler_params=pltpu.CompilerParams(collective_id=0, has_side_effects=True),
        name="spread_in",
    )(head_inputs, input_map, output_map, step_sizes, grad_output)

    state = shape((N, WIDE), F32)
    big = pltpu.CompilerParams(vmem_limit_bytes=48 * 1024 * 1024)
    fresh, message, ltok, lhead, dttok, f_out, m_out, d_out = pl.pallas_call(
        functools.partial(summary_kernel, ranks),
        out_shape=(
            shape((ranks, N, WIDE), F32),
            shape((ranks, N, WIDE), F32),
            shape((tokens, LANES), F32),
            shape((ranks, PER, SPAN), F32),
            shape((tokens, LANES), F32),
            state,
            state,
            shape((1, WIDE), F32),
        ),
        in_specs=[vmem] * 7,
        out_specs=(vmem,) * 8,
        compiler_params=big,
        name="summary",
    )(xg, bg, cg, dtg, dyg, rate, tok)

    def by_row(width):
        return pl.BlockSpec((SPAN, width), lambda k: (k, 0))

    per_block = pl.BlockSpec((1, PER, SPAN), lambda k: (k, 0, 0))
    u, agree, gb_l, gc_l = pl.pallas_call(
        local_kernel,
        grid=(ranks,),
        out_shape=(
            shape((tokens, WIDE), F32),
            shape((ranks, PER, SPAN), F32),
            shape((tokens, N), F32),
            shape((tokens, N), F32),
        ),
        in_specs=[
            by_row(WIDE),
            by_row(N),
            by_row(N),
            by_row(WIDE),
            by_row(LANES),
            per_block,
            by_row(LANES),
            by_row(4),
            pl.BlockSpec((1, SPAN), lambda k: (0, k)),
        ],
        out_specs=(by_row(WIDE), per_block, by_row(N), by_row(N)),
        compiler_params=big,
        cost_estimate=pl.CostEstimate(
            flops=8 * 10**9, bytes_accessed=8 * 10**6, transcendentals=10**6
        ),
        name="local",
    )(xg, bg, cg, dyg, ltok, lhead, dttok, tok, idrow)

    ahead = [(i, i + ranks) for i in range(contexts - ranks)]
    behind = [(i + ranks, i) for i in range(contexts - ranks)]
    s_move, a_move = f_out, m_out
    s_in = jnp.zeros_like(f_out)
    a_in = jnp.zeros_like(m_out)
    rounds = max(planes // 2, 1) if planes > 1 else 0
    for step in range(rounds):
        if step:
            s_move, a_move = d_out * s_move, d_out * a_move
        s_move = lax.ppermute(s_move, "context", ahead)
        a_move = lax.ppermute(a_move, "context", behind)
        s_in = s_in + s_move
        a_in = a_in + a_move

    gi, gs, gb, gc = pl.pallas_call(
        functools.partial(finish_kernel, ranks),
        out_shape=(
            shape((tokens, WIDE), BF),
            shape((ranks, PER, SPAN), F32),
            shape((tokens, N), F32),
            shape((tokens, N), F32),
        ),
        in_specs=[vmem] * 17,
        out_specs=(vmem,) * 4,
        scratch_shapes=[pltpu.VMEM((ranks + 1, N, WIDE), F32)],
        compiler_params=big,
        name="finish",
    )(
        xg, bg, cg, dyg, rate, tok, idrow, ltok, dttok, u, agree, gb_l, gc_l, fresh, message,
        s_in, a_in,
    )
    if ranks == 1:
        return gi, gs[0], gb, gc

    n_out = ranks * 4
    return pl.pallas_call(
        functools.partial(scatter_kernel, ranks),
        out_shape=(
            shape((SPAN, ranks * WIDE), BF),
            shape((heads_here, SPAN), F32),
            shape((SPAN, ranks * N), F32),
            shape((SPAN, ranks * N), F32),
        ),
        in_specs=[anywhere] * 4,
        out_specs=(anywhere,) * 4,
        scratch_shapes=[
            pltpu.SemaphoreType.DMA((n_out,)),
            pltpu.SemaphoreType.DMA((n_out,)),
            pltpu.SemaphoreType.DMA((4,)),
        ],
        compiler_params=pltpu.CompilerParams(collective_id=1, has_side_effects=True),
        name="spread_out",
    )(gi, gs, gb, gc)


def solution(mesh):
    placed = (
        P("context", "tensor"),
        P("tensor", "context"),
        P("tensor"),
        P("context", "tensor"),
        P("context", "tensor"),
        P("context"),
        P(("context", "tensor"), None),
    )
    return jax.shard_map(
        shards,
        mesh=mesh,
        in_specs=placed,
        out_specs=(
            P("context", "tensor"),
            P("tensor", "context"),
            P("context", "tensor"),
            P("context", "tensor"),
        ),
        check_vma=False,
    )
```

```python
import functools

import jax
import jax.numpy as jnp
from jax import lax
from jax.experimental import pallas as pl
from jax.experimental.pallas import tpu as pltpu
from jax.sharding import PartitionSpec as P

H = 128
P_SIZE = 64
N = 128
G = 8
SPAN = 128
PER = H // G
WIDE = PER * P_SIZE
LANES = 128
CHUNKS = 4
HC = PER // CHUNKS
CW = HC * P_SIZE
MESH = pl.DeviceIdType.MESH
BF = jnp.bfloat16
F32 = jnp.float32
NN = (((1,), (0,)), ((), ()))
NT = (((1,), (1,)), ((), ()))
TN = (((0,), (0,)), ((), ()))


def split(a):
    hi = a.astype(BF)
    return hi, (a - hi.astype(F32)).astype(BF)


def mm(a, b, dims=NN):
    return lax.dot_general(a, b, dims, preferred_element_type=F32)


def left2(a, b, dims=NN):
    hi, lo = split(a)
    return mm(hi, b, dims) + mm(lo, b, dims)


def right2(a, b, dims=NN):
    hi, lo = split(b)
    return mm(a, hi, dims) + mm(a, lo, dims)


def both3(a, b, dims=NN):
    ah, al = split(a)
    bh, bl = split(b)
    return mm(ah, bh, dims) + mm(ah, bl, dims) + mm(al, bh, dims)


def rows(k, size=SPAN):
    return pl.ds(k * size, size)


def mega_kernel(
    ranks, tensors, contexts, x, b, c, dt, dy, doc, rate, gi_o, gs_o, gb_o, gc_o,
    xg, dyg, bg, cg, dtg, docs, s_in, a_in, s_out, a_out, fresh, message, u, gi,
    tc, ltok, dttok, c_in, c_out, c_end, idcol, lhead, cross, neg, score, agree,
    dyy, xu, meets, gb, gc, gs,
    send_x, recv_x, send_dy, recv_dy, send_s, recv_s, send_doc, recv_doc,
    send_z, recv_z, send_o, recv_o, send_m, recv_m, local,
):
    planes = contexts // ranks
    last = planes - 1
    context = lax.axis_index("context")
    tensor = lax.axis_index("tensor")
    rank = lax.rem(context, ranks)
    base = context - rank
    plane = lax.div(context, ranks)
    part = dy.shape[0]
    spot = pl.multiple_of(rank * SPAN, SPAN)
    spot_dy = pl.multiple_of((rank * tensors + tensor) * part, part)

    barrier = pltpu.get_barrier_semaphore()
    for d in range(1, contexts):
        pl.semaphore_signal(
            barrier, inc=1,
            device_id={"context": lax.rem(context + d, contexts), "tensor": tensor},
            device_id_type=MESH,
        )
    for dr in range(ranks):
        for du in range(1, tensors):
            pl.semaphore_signal(
                barrier, inc=1,
                device_id={
                    "context": base + lax.rem(rank + dr, ranks),
                    "tensor": lax.rem(tensor + du, tensors),
                },
                device_id_type=MESH,
            )
    pl.semaphore_wait(barrier, contexts - 1 + ranks * (tensors - 1))

    def remote(src, dst, send, recv, ctx, ten):
        return pltpu.make_async_remote_copy(
            src_ref=src, dst_ref=dst, send_sem=send, recv_sem=recv,
            device_id={"context": ctx, "tensor": ten}, device_id_type=MESH,
        )

    def doc_copy(d):
        to = lax.rem(context + d, contexts)
        return remote(doc, docs.at[context], send_doc.at[d], recv_doc.at[d], to, tensor)

    def small_copies(dr):
        to = lax.rem(rank + dr, ranks)
        at = pl.multiple_of(to * N, N)
        pairs = [
            (dt.at[pl.ds(pl.multiple_of(to * PER, PER), PER), :], dtg.at[rank]),
            (b.at[:, pl.ds(at, N)], bg.at[pl.ds(spot, SPAN), :]),
            (c.at[:, pl.ds(at, N)], cg.at[pl.ds(spot, SPAN), :]),
        ]
        if dr == 0:
            return [pltpu.make_async_copy(s, d, local.at[n]) for n, (s, d) in enumerate(pairs)]
        return [
            remote(s, d, send_s.at[dr * 3 + n], recv_s.at[dr * 3 + n], base + to, tensor)
            for n, (s, d) in enumerate(pairs)
        ]

    def chunk_copies(ch):
        copies = []
        for dr in list(range(1, ranks)) + [0]:
            to = lax.rem(rank + dr, ranks)
            src = x.at[:, pl.ds(pl.multiple_of(to * WIDE + ch * CW, CW), CW)]
            dst = xg.at[ch, pl.ds(spot, SPAN), :]
            if dr == 0:
                copies.append(pltpu.make_async_copy(src, dst, recv_x.at[ch, 0]))
            else:
                copies.append(
                    remote(src, dst, send_x.at[ch, dr], recv_x.at[ch, dr], base + to, tensor)
                )
            for du in range(tensors):
                tt = lax.rem(tensor + du, tensors)
                at = pl.multiple_of((tt * ranks + to) * WIDE + ch * CW, CW)
                src, dst = dy.at[:, pl.ds(at, CW)], dyg.at[ch, pl.ds(spot_dy, part), :]
                n = dr * tensors + du
                if n == 0:
                    copies.append(pltpu.make_async_copy(src, dst, recv_dy.at[ch, 0]))
                else:
                    copies.append(
                        remote(src, dst, send_dy.at[ch, n], recv_dy.at[ch, n], base + to, tt)
                    )
        return copies

    def wait_in(copy):
        if copy.is_remote:
            copy.wait_recv()
        else:
            copy.wait()

    own_doc = pltpu.make_async_copy(doc, docs.at[context], local.at[3])
    own_doc.start()
    for dr in list(range(1, ranks)) + [0]:
        for copy in small_copies(dr):
            copy.start()
    for d in range(1, contexts):
        doc_copy(d).start()
    for ch in range(CHUNKS):
        for copy in chunk_copies(ch):
            copy.start()

    @pl.when(plane == 0)
    def _():
        s_in[...] = jnp.zeros_like(s_in)

    @pl.when(plane == last)
    def _():
        a_in[...] = jnp.zeros_like(a_in)

    score[...] = jnp.zeros_like(score)
    dyy[...] = jnp.zeros_like(dyy)
    xu[...] = jnp.zeros_like(xu)
    meets[...] = jnp.zeros_like(meets)
    gb[...] = jnp.zeros_like(gb)
    gc[...] = jnp.zeros_like(gc)

    row_i = lax.broadcasted_iota(jnp.int32, (SPAN, SPAN), 0)
    col_i = lax.broadcasted_iota(jnp.int32, (SPAN, SPAN), 1)
    ordered = row_i <= col_i
    up = ordered.astype(F32)
    pad = jnp.zeros((LANES - PER, SPAN), F32)

    own_doc.wait()
    for d in range(1, contexts):
        doc_copy(d).wait_recv()
    for dr in list(range(1, ranks)) + [0]:
        for copy in small_copies(dr):
            wait_in(copy)
    before = docs[jnp.maximum(base - 1, 0)][:, SPAN - 1 :]
    before = jnp.where(plane == 0, -1.0, before)
    after = docs[jnp.minimum(base + ranks, contexts - 1)][:, :1]
    after = jnp.where(plane == last, -1.0, after)
    id_rows = [docs[base + k] for k in range(ranks)]
    for k in range(ranks):
        at = rows(k)
        id_row = id_rows[k]
        prev_id = id_rows[k - 1][:, SPAN - 1 :] if k else before
        next_id = id_rows[k + 1][:, :1] if k + 1 < ranks else after
        ids = jnp.transpose(jnp.broadcast_to(id_row, (SPAN, SPAN)))
        idcol[k] = ids
        steps = dtg[k]
        cum = lax.dot_general(
            -rate[...] * steps, up, NN, precision=lax.Precision.HIGHEST, preferred_element_type=F32
        )
        cum_t = jnp.transpose(jnp.concatenate([cum, pad], axis=0))
        dt_t = jnp.transpose(jnp.concatenate([steps, pad], axis=0))
        ltok[at, :] = cum_t
        dttok[at, :] = dt_t
        for ch in range(CHUNKS):
            mine = slice(ch * HC, (ch + 1) * HC)
            both = jnp.concatenate([cum[mine], steps[mine]], axis=0)
            lhead[ch, k] = both
            tc[ch, at, :] = jnp.transpose(
                jnp.concatenate([both, jnp.zeros((LANES - 2 * HC, SPAN), F32)], axis=0)
            )
        rest = jnp.exp(cum_t[SPAN - 1 :, :] - cum_t)
        c_in[at, :] = jnp.where(ids == prev_id, jnp.exp(cum_t), 0.0)
        c_out[at, :] = jnp.where(ids == next_id, rest, 0.0)
        c_end[at, :] = jnp.where(ids == id_row[:, SPAN - 1 :], rest, 0.0) * dt_t
        neg[k] = jnp.where(ordered & (ids == id_row), 0.0, -1e30)
        cross[k] = mm(bg[at, :], cg[at, :], NT)

    lane_row = lax.broadcasted_iota(jnp.int32, (LANES, CW), 0)
    lane_col = lax.broadcasted_iota(jnp.int32, (LANES, CW), 1) // P_SIZE

    def spread_of(ch):
        return jnp.where(lane_row == lane_col + ch * HC, 1.0, 0.0).astype(BF)

    def decay_of(k, spread):
        return left2(c_in[k * SPAN + SPAN - 8 : (k + 1) * SPAN, :], spread)[7:, :]

    def summarise(ch):
        for copy in chunk_copies(ch):
            wait_in(copy)
        spread = spread_of(ch)
        for k in range(ranks):
            at = rows(k)
            xs = xg[ch, at, :].astype(F32) * left2(c_end[at, :], spread)
            dyc = dyg[ch, at, :].astype(F32) * left2(c_in[at, :], spread)
            fresh[ch, k] = right2(bg[at, :], xs, TN)
            message[ch, k] = right2(cg[at, :], dyc, TN)

    def s_copy(ch):
        return remote(
            s_out.at[ch], s_in.at[ch], send_z.at[0, ch], recv_z.at[0, ch],
            jnp.minimum(context + ranks, contexts - 1), tensor,
        )

    def a_copy(ch):
        return remote(
            a_out.at[ch], a_in.at[ch], send_z.at[1, ch], recv_z.at[1, ch],
            jnp.maximum(context - ranks, 0), tensor,
        )

    def pass_state(ch):
        @pl.when(plane > 0)
        def _():
            s_copy(ch).wait_recv()

        @pl.when(plane < last)
        def _():
            spread = spread_of(ch)
            state = s_in[ch]
            for k in range(ranks):
                state = decay_of(k, spread) * state + fresh[ch, k]
            s_out[ch] = state
            s_copy(ch).start()

    def pass_adjoint(ch):
        @pl.when(plane < last)
        def _():
            a_copy(ch).wait_recv()

        @pl.when(plane > 0)
        def _():
            spread = spread_of(ch)
            state = a_in[ch]
            for k in range(ranks - 1, -1, -1):
                state = decay_of(k, spread) * state + message[ch, k]
            a_out[ch] = state
            a_copy(ch).start()

    def inside(ch):
        def block(k, carry):
            at = pl.ds(pl.multiple_of(k * SPAN, SPAN), SPAN)
            cross_t = cross[k]
            hide = neg[k]
            total = score[k]
            x_k, dy_k, cols, heads = xg[ch, at, :], dyg[ch, at, :], tc[ch, at, :], lhead[ch, k]
            agrees = []
            for h in range(HC):
                cut = slice(h * P_SIZE, (h + 1) * P_SIZE)
                x_h, dy_h = x_k[:, cut], dy_k[:, cut]
                w = jnp.exp((heads[h : h + 1, :] - cols[:, h : h + 1]) + hide)
                u[ch, at, cut] = left2(w * cross_t, dy_h)
                q = w * mm(x_h, dy_h, NT) * cols[:, HC + h : HC + h + 1]
                total = total + q
                agrees.append(jnp.sum(q * cross_t, axis=0, keepdims=True))
            score[k] = total
            agree[ch, k] = jnp.concatenate(agrees + agrees, axis=0)
            return carry

        lax.fori_loop(0, ranks, block, 0)

    def gi_copies(ch):
        copies = []
        for dr in list(range(1, ranks)) + [0]:
            to = lax.rem(rank + dr, ranks)
            src = gi.at[ch, pl.ds(pl.multiple_of(to * SPAN, SPAN), SPAN), :]
            dst = gi_o.at[:, pl.ds(pl.multiple_of(rank * WIDE + ch * CW, CW), CW)]
            if dr == 0:
                copies.append(pltpu.make_async_copy(src, dst, recv_o.at[ch, 0]))
            else:
                copies.append(
                    remote(src, dst, send_o.at[ch, dr], recv_o.at[ch, dr], base + to, tensor)
                )
        return copies

    def finish(ch):
        spread = spread_of(ch)
        states = [s_in[ch]]
        for k in range(ranks):
            states.append(decay_of(k, spread) * states[k] + fresh[ch, k])
        adj = a_in[ch]
        for k in range(ranks - 1, -1, -1):
            at = rows(k)
            in_e = left2(c_in[at, :], spread)
            out_e = left2(c_out[at, :], spread)
            dt_e = left2(dttok[at, :], spread)
            state = states[k]
            x_f = xg[ch, at, :].astype(F32)
            dyc = dyg[ch, at, :].astype(F32) * in_e
            total_u = u[ch, at, :] + right2(bg[at, :], adj) * out_e
            gi[ch, at, :] = (total_u * dt_e).astype(BF)
            gc[at, :] += both3(dyc, state, NT)
            gb[at, :] += both3(x_f * out_e * dt_e, adj, NT)
            dyy[at, :] += left2(dyc * right2(cg[at, :], state), spread, NT)
            xu[at, :] += left2(x_f * total_u, spread, NT)
            meet = jnp.sum(states[k + 1] * adj, axis=0, keepdims=True)
            meets[k] += left2(jnp.broadcast_to(meet, (8, CW)), spread, NT)
            adj = in_e[SPAN - 1 :, :] * adj + message[ch, k]
        for copy in gi_copies(ch):
            copy.start()

    def step(it, carry):
        @pl.when(it < CHUNKS)
        def _():
            summarise(it)

        ahead = it - plane

        @pl.when((ahead >= 0) & (ahead < CHUNKS))
        def _():
            pass_state(ahead)

        behind = it - (last - plane)

        @pl.when((behind >= 0) & (behind < CHUNKS))
        def _():
            pass_adjoint(behind)

        @pl.when(it < CHUNKS)
        def _():
            inside(it)

        @pl.when(it >= last)
        def _():
            finish(it - last)

        return carry

    lax.fori_loop(0, CHUNKS + last, step, 0)

    rate_row = jnp.transpose(
        jnp.concatenate([jnp.broadcast_to(rate[...], (PER, SPAN)), pad], axis=0)
    )
    for k in range(ranks):
        at = rows(k)
        id_row = id_rows[k]
        next_id = id_rows[k + 1][:, :1] if k + 1 < ranks else after
        ids = idcol[k]
        gb[at, :] += left2(score[k], cg[at, :])
        gc[at, :] += left2(score[k], bg[at, :], TN)
        agree_k = jnp.concatenate([agree[ch, k][:HC] for ch in range(CHUNKS)] + [pad], axis=0)
        slope = jnp.transpose(agree_k) + dyy[at, :] - dttok[at, :] * xu[at, :]
        same = jnp.where((ids == id_row) & ordered, 1.0, 0.0).astype(BF)
        tails = right2(same, slope) + jnp.where(ids == next_id, meets[k][:1], 0.0)
        gs[k] = jnp.transpose(xu[at, :] - rate_row * tails)[:PER, :]

    def map_copies(dr):
        to = lax.rem(rank + dr, ranks)
        there = pl.ds(pl.multiple_of(to * SPAN, SPAN), SPAN)
        at = pl.ds(pl.multiple_of(rank * N, N), N)
        pairs = [
            (gb.at[there, :], gb_o.at[:, at]),
            (gc.at[there, :], gc_o.at[:, at]),
            (gs.at[to], gs_o.at[pl.ds(pl.multiple_of(rank * PER, PER), PER), :]),
        ]
        if dr == 0:
            return [pltpu.make_async_copy(s, d, local.at[n]) for n, (s, d) in enumerate(pairs)]
        return [
            remote(s, d, send_m.at[dr * 3 + n], recv_m.at[dr * 3 + n], base + to, tensor)
            for n, (s, d) in enumerate(pairs)
        ]

    order = list(range(1, ranks)) + [0]
    for dr in order:
        for copy in map_copies(dr):
            copy.start()
    for d in range(1, contexts):
        doc_copy(d).wait_send()
    for dr in order[:-1]:
        for copy in small_copies(dr):
            copy.wait_send()
    for ch in range(CHUNKS):
        for copy in chunk_copies(ch):
            if copy.is_remote:
                copy.wait_send()
        for copy in gi_copies(ch):
            copy.wait()

        @pl.when(plane < last)
        def _():
            s_copy(ch).wait_send()

        @pl.when(plane > 0)
        def _():
            a_copy(ch).wait_send()

    for dr in order:
        for copy in map_copies(dr):
            copy.wait()


def shards(head_inputs, step_sizes, decay_rate, input_map, output_map, document, grad_output):
    heads_here = decay_rate.shape[0]
    ranks = heads_here // PER
    contexts = lax.axis_size("context")
    tensors = lax.axis_size("tensor")
    tokens = ranks * SPAN
    rank = lax.axis_index("context") % ranks
    anywhere = pl.BlockSpec(memory_space=pl.ANY)
    vmem = pl.BlockSpec(memory_space=pltpu.VMEM)
    shape = jax.ShapeDtypeStruct
    mem = pltpu.VMEM
    dma = pltpu.SemaphoreType.DMA
    doc = document.astype(F32)[None, :]
    rate = lax.dynamic_slice(decay_rate, (rank * PER,), (PER,))[:, None]
    return pl.pallas_call(
        functools.partial(mega_kernel, ranks, tensors, contexts),
        out_shape=(
            shape((SPAN, ranks * WIDE), BF),
            shape((heads_here, SPAN), F32),
            shape((SPAN, ranks * N), F32),
            shape((SPAN, ranks * N), F32),
        ),
        in_specs=[anywhere] * 5 + [vmem] * 2,
        out_specs=(anywhere,) * 4,
        scratch_shapes=[
            mem((CHUNKS, tokens, CW), BF),
            mem((CHUNKS, tokens, CW), BF),
            mem((tokens, N), BF),
            mem((tokens, N), BF),
            mem((ranks, PER, SPAN), F32),
            mem((contexts, 1, SPAN), F32),
            mem((CHUNKS, N, CW), F32),
            mem((CHUNKS, N, CW), F32),
            mem((CHUNKS, N, CW), F32),
            mem((CHUNKS, N, CW), F32),
            mem((CHUNKS, ranks, N, CW), F32),
            mem((CHUNKS, ranks, N, CW), F32),
            mem((CHUNKS, tokens, CW), F32),
            mem((CHUNKS, tokens, CW), BF),
            mem((CHUNKS, tokens, LANES), F32),
            mem((tokens, LANES), F32),
            mem((tokens, LANES), F32),
            mem((tokens, LANES), F32),
            mem((tokens, LANES), F32),
            mem((tokens, LANES), F32),
            mem((ranks, SPAN, SPAN), F32),
            mem((CHUNKS, ranks, 2 * HC, SPAN), F32),
            mem((ranks, SPAN, SPAN), F32),
            mem((ranks, SPAN, SPAN), F32),
            mem((ranks, SPAN, SPAN), F32),
            mem((CHUNKS, ranks, 2 * HC, SPAN), F32),
            mem((tokens, LANES), F32),
            mem((tokens, LANES), F32),
            mem((ranks, 8, LANES), F32),
            mem((tokens, N), F32),
            mem((tokens, N), F32),
            mem((ranks, PER, SPAN), F32),
            dma((CHUNKS, ranks)),
            dma((CHUNKS, ranks)),
            dma((CHUNKS, ranks * tensors)),
            dma((CHUNKS, ranks * tensors)),
            dma((ranks * 3,)),
            dma((ranks * 3,)),
            dma((contexts,)),
            dma((contexts,)),
            dma((2, CHUNKS)),
            dma((2, CHUNKS)),
            dma((CHUNKS, ranks)),
            dma((CHUNKS, ranks)),
            dma((ranks * 3,)),
            dma((ranks * 3,)),
            dma((4,)),
        ],
        compiler_params=pltpu.CompilerParams(
            collective_id=0, has_side_effects=True, vmem_limit_bytes=48 * 1024 * 1024
        ),
        name="mixer",
    )(head_inputs, input_map, output_map, step_sizes, grad_output, doc, rate)


def solution(mesh):
    placed = (
        P("context", "tensor"),
        P("tensor", "context"),
        P("tensor"),
        P("context", "tensor"),
        P("context", "tensor"),
        P("context"),
        P(("context", "tensor"), None),
    )
    return jax.shard_map(
        shards,
        mesh=mesh,
        in_specs=placed,
        out_specs=(
            P("context", "tensor"),
            P("tensor", "context"),
            P("context", "tensor"),
            P("context", "tensor"),
        ),
        check_vma=False,
    )
```

```python
import functools

import jax
import jax.numpy as jnp
from jax import lax
from jax.experimental import pallas as pl
from jax.experimental.pallas import tpu as pltpu
from jax.sharding import PartitionSpec as P

H = 128
P_SIZE = 64
N = 128
G = 8
SPAN = 128
PER = H // G
WIDE = PER * P_SIZE
LANES = 128
CHUNKS = 4
HC = PER // CHUNKS
CW = HC * P_SIZE
MESH = pl.DeviceIdType.MESH
BF = jnp.bfloat16
F32 = jnp.float32
NN = (((1,), (0,)), ((), ()))
NT = (((1,), (1,)), ((), ()))
TN = (((0,), (0,)), ((), ()))


def split(a):
    hi = a.astype(BF)
    return hi, (a - hi.astype(F32)).astype(BF)


def mm(a, b, dims=NN):
    return lax.dot_general(a, b, dims, preferred_element_type=F32)


def left2(a, b, dims=NN):
    hi, lo = split(a)
    return mm(hi, b, dims) + mm(lo, b, dims)


def right2(a, b, dims=NN):
    hi, lo = split(b)
    return mm(a, hi, dims) + mm(a, lo, dims)


def both3(a, b, dims=NN):
    ah, al = split(a)
    bh, bl = split(b)
    return mm(ah, bh, dims) + mm(ah, bl, dims) + mm(al, bh, dims)


def rows(k, size=SPAN):
    return pl.ds(k * size, size)


def mega_kernel(
    ranks, tensors, contexts, x, b, c, dt, dy, doc, rate_in, gi_o, gs_o, gb_o, gc_o,
    xg, dyg, bg, cg, dtg, docs, rates, s_in, a_in, s_out, a_out, fresh, message, decays, u, gi,
    tc, ltok, dttok, c_in, c_out, c_end, idcol, lhead, cross, neg, score, agree,
    dyy, xu, meets, gb, gc, gs,
    send_x, recv_x, send_dy, recv_dy, send_s, recv_s, send_doc, recv_doc,
    send_z, recv_z, send_o, recv_o, send_m, recv_m, local,
):
    planes = contexts // ranks
    last = planes - 1
    context = lax.axis_index("context")
    tensor = lax.axis_index("tensor")
    rank = lax.rem(context, ranks)
    base = context - rank
    plane = lax.div(context, ranks)
    part = dy.shape[0]
    spot = pl.multiple_of(rank * SPAN, SPAN)
    spot_dy = pl.multiple_of((rank * tensors + tensor) * part, part)

    barrier = pltpu.get_barrier_semaphore()
    for d in range(1, contexts):
        pl.semaphore_signal(
            barrier, inc=1,
            device_id={"context": lax.rem(context + d, contexts), "tensor": tensor},
            device_id_type=MESH,
        )
    for dr in range(ranks):
        for du in range(1, tensors):
            pl.semaphore_signal(
                barrier, inc=1,
                device_id={
                    "context": base + lax.rem(rank + dr, ranks),
                    "tensor": lax.rem(tensor + du, tensors),
                },
                device_id_type=MESH,
            )
    pl.semaphore_wait(barrier, contexts - 1 + ranks * (tensors - 1))

    def remote(src, dst, send, recv, ctx, ten):
        return pltpu.make_async_remote_copy(
            src_ref=src, dst_ref=dst, send_sem=send, recv_sem=recv,
            device_id={"context": ctx, "tensor": ten}, device_id_type=MESH,
        )

    def doc_copy(d):
        to = lax.rem(context + d, contexts)
        return remote(doc, docs.at[context], send_doc.at[d], recv_doc.at[d], to, tensor)

    def small_copies(dr):
        to = lax.rem(rank + dr, ranks)
        at = pl.multiple_of(to * N, N)
        pairs = [
            (dt.at[pl.ds(pl.multiple_of(to * PER, PER), PER), :], dtg.at[rank]),
            (b.at[:, pl.ds(at, N)], bg.at[pl.ds(spot, SPAN), :]),
            (c.at[:, pl.ds(at, N)], cg.at[pl.ds(spot, SPAN), :]),
        ]
        if dr == 0:
            return [pltpu.make_async_copy(s, d, local.at[n]) for n, (s, d) in enumerate(pairs)]
        return [
            remote(s, d, send_s.at[dr * 3 + n], recv_s.at[dr * 3 + n], base + to, tensor)
            for n, (s, d) in enumerate(pairs)
        ]

    def chunk_copies(ch):
        copies = []
        for dr in list(range(1, ranks)) + [0]:
            to = lax.rem(rank + dr, ranks)
            src = x.at[:, pl.ds(pl.multiple_of(to * WIDE + ch * CW, CW), CW)]
            dst = xg.at[ch, pl.ds(spot, SPAN), :]
            if dr == 0:
                copies.append(pltpu.make_async_copy(src, dst, recv_x.at[ch, 0]))
            else:
                copies.append(
                    remote(src, dst, send_x.at[ch, dr], recv_x.at[ch, dr], base + to, tensor)
                )
            for du in range(tensors):
                tt = lax.rem(tensor + du, tensors)
                at = pl.multiple_of((tt * ranks + to) * WIDE + ch * CW, CW)
                src, dst = dy.at[:, pl.ds(at, CW)], dyg.at[ch, pl.ds(spot_dy, part), :]
                n = dr * tensors + du
                if n == 0:
                    copies.append(pltpu.make_async_copy(src, dst, recv_dy.at[ch, 0]))
                else:
                    copies.append(
                        remote(src, dst, send_dy.at[ch, n], recv_dy.at[ch, n], base + to, tt)
                    )
        return copies

    def wait_in(copy):
        if copy.is_remote:
            copy.wait_recv()
        else:
            copy.wait()

    own_doc = pltpu.make_async_copy(doc, docs.at[context], local.at[3])
    own_doc.start()
    for dr in list(range(1, ranks)) + [0]:
        for copy in small_copies(dr):
            copy.start()
    for d in range(1, contexts):
        doc_copy(d).start()
    for ch in range(CHUNKS):
        for copy in chunk_copies(ch):
            copy.start()

    @pl.when(plane == 0)
    def _():
        s_in[...] = jnp.zeros_like(s_in)

    @pl.when(plane == last)
    def _():
        a_in[...] = jnp.zeros_like(a_in)

    score[...] = jnp.zeros_like(score)
    dyy[...] = jnp.zeros_like(dyy)
    xu[...] = jnp.zeros_like(xu)
    meets[...] = jnp.zeros_like(meets)
    gb[...] = jnp.zeros_like(gb)
    gc[...] = jnp.zeros_like(gc)

    row_i = lax.broadcasted_iota(jnp.int32, (SPAN, SPAN), 0)
    col_i = lax.broadcasted_iota(jnp.int32, (SPAN, SPAN), 1)
    ordered = row_i <= col_i
    up = ordered.astype(F32)
    pad = jnp.zeros((LANES - PER, SPAN), F32)

    heads = rate_in.shape[1]
    rate_wide = rate_in[...]
    if heads < LANES:
        rate_wide = jnp.concatenate([rate_wide, jnp.zeros((1, LANES - heads), F32)], axis=1)
    rates[...] = jnp.transpose(jnp.broadcast_to(rate_wide, (LANES, LANES)))
    rate = rates[pl.ds(pl.multiple_of(rank * PER, PER), PER), :]

    own_doc.wait()
    for d in range(1, contexts):
        doc_copy(d).wait_recv()
    for dr in list(range(1, ranks)) + [0]:
        for copy in small_copies(dr):
            wait_in(copy)
    before = docs[jnp.maximum(base - 1, 0)].astype(F32)[:, SPAN - 1 :]
    before = jnp.where(plane == 0, -1.0, before)
    after = docs[jnp.minimum(base + ranks, contexts - 1)].astype(F32)[:, :1]
    after = jnp.where(plane == last, -1.0, after)
    id_rows = [docs[base + k].astype(F32) for k in range(ranks)]
    for k in range(ranks):
        at = rows(k)
        id_row = id_rows[k]
        prev_id = id_rows[k - 1][:, SPAN - 1 :] if k else before
        next_id = id_rows[k + 1][:, :1] if k + 1 < ranks else after
        ids = jnp.transpose(jnp.broadcast_to(id_row, (SPAN, SPAN)))
        idcol[k] = ids
        steps = dtg[k]
        cum = lax.dot_general(
            -rate * steps, up, NN, precision=lax.Precision.HIGHEST, preferred_element_type=F32
        )
        cum_t = jnp.transpose(jnp.concatenate([cum, pad], axis=0))
        dt_t = jnp.transpose(jnp.concatenate([steps, pad], axis=0))
        ltok[at, :] = cum_t
        dttok[at, :] = dt_t
        for ch in range(CHUNKS):
            mine = slice(ch * HC, (ch + 1) * HC)
            both = jnp.concatenate([cum[mine], steps[mine]], axis=0)
            lhead[ch, k] = both
            tc[ch, at, :] = jnp.transpose(
                jnp.concatenate([both, jnp.zeros((LANES - 2 * HC, SPAN), F32)], axis=0)
            )
        rest = jnp.exp(cum_t[SPAN - 1 :, :] - cum_t)
        c_in[at, :] = jnp.where(ids == prev_id, jnp.exp(cum_t), 0.0)
        c_out[at, :] = jnp.where(ids == next_id, rest, 0.0)
        c_end[at, :] = jnp.where(ids == id_row[:, SPAN - 1 :], rest, 0.0) * dt_t
        neg[k] = jnp.where(ordered & (ids == id_row), 0.0, -1e30)
        cross[k] = mm(bg[at, :], cg[at, :], NT)

    lane_row = lax.broadcasted_iota(jnp.int32, (LANES, CW), 0)
    lane_col = lax.broadcasted_iota(jnp.int32, (LANES, CW), 1) // P_SIZE

    def spread_of(ch):
        return jnp.where(lane_row == lane_col + ch * HC, 1.0, 0.0).astype(BF)

    def summarise(ch):
        for copy in chunk_copies(ch):
            wait_in(copy)
        spread = spread_of(ch)
        for k in range(ranks):
            at = rows(k)
            xs = xg[ch, at, :].astype(F32) * left2(c_end[at, :], spread)
            in_e = left2(c_in[at, :], spread)
            dyc = dyg[ch, at, :].astype(F32) * in_e
            decays[ch, k] = in_e[SPAN - 1 :, :]
            fresh[ch, k] = right2(bg[at, :], xs, TN)
            message[ch, k] = right2(cg[at, :], dyc, TN)
        state = fresh[ch, 0]
        decay = decays[ch, 0]
        for k in range(1, ranks):
            state = decays[ch, k] * state + fresh[ch, k]
            decay = decays[ch, k] * decay
        s_out[ch] = state
        state = message[ch, ranks - 1]
        for k in range(ranks - 2, -1, -1):
            state = decays[ch, k] * state + message[ch, k]
        a_out[ch] = state
        decays[ch, ranks] = decay

    def s_copy(ch):
        return remote(
            s_out.at[ch], s_in.at[ch], send_z.at[0, ch], recv_z.at[0, ch],
            jnp.minimum(context + ranks, contexts - 1), tensor,
        )

    def a_copy(ch):
        return remote(
            a_out.at[ch], a_in.at[ch], send_z.at[1, ch], recv_z.at[1, ch],
            jnp.maximum(context - ranks, 0), tensor,
        )

    def pass_state(ch):
        @pl.when(plane > 0)
        def _():
            s_copy(ch).wait_recv()

        @pl.when(plane < last)
        def _():
            s_out[ch] += decays[ch, ranks] * s_in[ch]
            s_copy(ch).start()

    def pass_adjoint(ch):
        @pl.when(plane < last)
        def _():
            a_copy(ch).wait_recv()

        @pl.when(plane > 0)
        def _():
            a_out[ch] += decays[ch, ranks] * a_in[ch]
            a_copy(ch).start()

    def inside(ch):
        def block(k, carry):
            at = pl.ds(pl.multiple_of(k * SPAN, SPAN), SPAN)
            cross_t = cross[k]
            hide = neg[k]
            total = score[k]
            x_k, dy_k, cols, heads = xg[ch, at, :], dyg[ch, at, :], tc[ch, at, :], lhead[ch, k]
            agrees = []
            for h in range(HC):
                cut = slice(h * P_SIZE, (h + 1) * P_SIZE)
                x_h, dy_h = x_k[:, cut], dy_k[:, cut]
                w = jnp.exp((heads[h : h + 1, :] - cols[:, h : h + 1]) + hide)
                u[ch, at, cut] = left2(w * cross_t, dy_h)
                q = w * mm(x_h, dy_h, NT) * cols[:, HC + h : HC + h + 1]
                total = total + q
                agrees.append(jnp.sum(q * cross_t, axis=0, keepdims=True))
            score[k] = total
            agree[ch, k] = jnp.concatenate(agrees, axis=0)
            return carry

        lax.fori_loop(0, ranks, block, 0)

    def gi_pair(ch, to):
        return (
            gi.at[ch, pl.ds(to * SPAN, SPAN), :],
            gi_o.at[:, pl.ds(pl.multiple_of(rank * WIDE + ch * CW, CW), CW)],
        )

    def gi_local(ch, to):
        return pltpu.make_async_copy(*gi_pair(ch, to), recv_o.at[ch, rank])

    def gi_remote(ch, to):
        return remote(
            *gi_pair(ch, to), send_o.at[ch, to], recv_o.at[ch, rank], base + to, tensor
        )

    def gi_start(ch, to):
        @pl.when(rank == to)
        def _():
            gi_local(ch, to).start()

        @pl.when(rank != to)
        def _():
            gi_remote(ch, to).start()

    def gi_wait(ch, other):
        @pl.when(rank == other)
        def _():
            gi_local(ch, other).wait()

        @pl.when(rank != other)
        def _():
            remote(
                *gi_pair(ch, other), send_o.at[ch, other], recv_o.at[ch, other], base + other, tensor
            ).wait()

    def finish(ch):
        spread = spread_of(ch)
        states = [s_in[ch]]
        for k in range(ranks):
            states.append(decays[ch, k] * states[k] + fresh[ch, k])
        adj = a_in[ch]
        for k in range(ranks - 1, -1, -1):
            at = rows(k)
            in_e = left2(c_in[at, :], spread)
            out_e = left2(c_out[at, :], spread)
            dt_e = left2(dttok[at, :], spread)
            state = states[k]
            x_f = xg[ch, at, :].astype(F32)
            dyc = dyg[ch, at, :].astype(F32) * in_e
            total_u = u[ch, at, :] + right2(bg[at, :], adj) * out_e
            gi[ch, at, :] = (total_u * dt_e).astype(BF)
            gi_start(ch, k)
            gc[at, :] += both3(dyc, state, NT)
            gb[at, :] += both3(x_f * out_e * dt_e, adj, NT)
            dyy[at, :] += left2(dyc * right2(cg[at, :], state), spread, NT)
            xu[at, :] += left2(x_f * total_u, spread, NT)
            meet = jnp.sum(states[k + 1] * adj, axis=0, keepdims=True)
            meets[k] += left2(jnp.broadcast_to(meet, (8, CW)), spread, NT)
            adj = decays[ch, k] * adj + message[ch, k]
    def step(it, carry):
        @pl.when(it < CHUNKS)
        def _():
            summarise(it)

        ahead = it - plane

        @pl.when((ahead >= 0) & (ahead < CHUNKS))
        def _():
            pass_state(ahead)

        behind = it - (last - plane)

        @pl.when((behind >= 0) & (behind < CHUNKS))
        def _():
            pass_adjoint(behind)

        @pl.when(it < CHUNKS)
        def _():
            inside(it)

        @pl.when(it >= last)
        def _():
            finish(it - last)

        return carry

    lax.fori_loop(0, CHUNKS + last, step, 0)

    rate_row = jnp.transpose(
        jnp.concatenate([rates[pl.ds(pl.multiple_of(rank * PER, PER), PER), :], pad], axis=0)
    )
    for k in range(ranks):
        at = rows(k)
        id_row = id_rows[k]
        next_id = id_rows[k + 1][:, :1] if k + 1 < ranks else after
        ids = idcol[k]
        gb[at, :] += left2(score[k], cg[at, :])
        gc[at, :] += left2(score[k], bg[at, :], TN)
        agree_k = jnp.concatenate([agree[ch, k] for ch in range(CHUNKS)] + [pad], axis=0)
        slope = jnp.transpose(agree_k) + dyy[at, :] - dttok[at, :] * xu[at, :]
        same = jnp.where((ids == id_row) & ordered, 1.0, 0.0).astype(BF)
        tails = right2(same, slope) + jnp.where(ids == next_id, meets[k][:1], 0.0)
        gs[k] = jnp.transpose(xu[at, :] - rate_row * tails)[:PER, :]

    def map_copies(dr):
        to = lax.rem(rank + dr, ranks)
        there = pl.ds(pl.multiple_of(to * SPAN, SPAN), SPAN)
        at = pl.ds(pl.multiple_of(rank * N, N), N)
        pairs = [
            (gb.at[there, :], gb_o.at[:, at]),
            (gc.at[there, :], gc_o.at[:, at]),
            (gs.at[to], gs_o.at[pl.ds(pl.multiple_of(rank * PER, PER), PER), :]),
        ]
        if dr == 0:
            return [pltpu.make_async_copy(s, d, local.at[n]) for n, (s, d) in enumerate(pairs)]
        return [
            remote(s, d, send_m.at[dr * 3 + n], recv_m.at[dr * 3 + n], base + to, tensor)
            for n, (s, d) in enumerate(pairs)
        ]

    order = list(range(1, ranks)) + [0]
    for dr in order:
        for copy in map_copies(dr):
            copy.start()
    for d in range(1, contexts):
        doc_copy(d).wait_send()
    for dr in order[:-1]:
        for copy in small_copies(dr):
            copy.wait_send()
    for ch in range(CHUNKS):
        for copy in chunk_copies(ch):
            if copy.is_remote:
                copy.wait_send()
        for other in range(ranks):
            gi_wait(ch, other)

        @pl.when(plane < last)
        def _():
            s_copy(ch).wait_send()

        @pl.when(plane > 0)
        def _():
            a_copy(ch).wait_send()

    for dr in order:
        for copy in map_copies(dr):
            copy.wait()


def shards(head_inputs, step_sizes, decay_rate, input_map, output_map, document, grad_output):
    heads_here = decay_rate.shape[0]
    ranks = heads_here // PER
    contexts = lax.axis_size("context")
    tensors = lax.axis_size("tensor")
    tokens = ranks * SPAN
    hbm = pl.BlockSpec(memory_space=pltpu.HBM)
    vmem = pl.BlockSpec(memory_space=pltpu.VMEM)
    shape = jax.ShapeDtypeStruct
    mem = pltpu.VMEM
    dma = pltpu.SemaphoreType.DMA
    return pl.pallas_call(
        functools.partial(mega_kernel, ranks, tensors, contexts),
        out_shape=(
            shape((SPAN, ranks * WIDE), BF),
            shape((heads_here, SPAN), F32),
            shape((SPAN, ranks * N), F32),
            shape((SPAN, ranks * N), F32),
        ),
        in_specs=[hbm] * 5 + [vmem] * 2,
        out_specs=(hbm,) * 4,
        scratch_shapes=[
            mem((CHUNKS, tokens, CW), BF),
            mem((CHUNKS, tokens, CW), BF),
            mem((tokens, N), BF),
            mem((tokens, N), BF),
            mem((ranks, PER, SPAN), F32),
            mem((contexts, 1, SPAN), jnp.int32),
            mem((LANES, LANES), F32),
            mem((CHUNKS, N, CW), F32),
            mem((CHUNKS, N, CW), F32),
            mem((CHUNKS, N, CW), F32),
            mem((CHUNKS, N, CW), F32),
            mem((CHUNKS, ranks, N, CW), F32),
            mem((CHUNKS, ranks, N, CW), F32),
            mem((CHUNKS, ranks + 1, 1, CW), F32),
            mem((CHUNKS, tokens, CW), F32),
            mem((CHUNKS, tokens, CW), BF),
            mem((CHUNKS, tokens, LANES), F32),
            mem((tokens, LANES), F32),
            mem((tokens, LANES), F32),
            mem((tokens, LANES), F32),
            mem((tokens, LANES), F32),
            mem((tokens, LANES), F32),
            mem((ranks, SPAN, SPAN), F32),
            mem((CHUNKS, ranks, 2 * HC, SPAN), F32),
            mem((ranks, SPAN, SPAN), F32),
            mem((ranks, SPAN, SPAN), F32),
            mem((ranks, SPAN, SPAN), F32),
            mem((CHUNKS, ranks, HC, SPAN), F32),
            mem((tokens, LANES), F32),
            mem((tokens, LANES), F32),
            mem((ranks, 8, LANES), F32),
            mem((tokens, N), F32),
            mem((tokens, N), F32),
            mem((ranks, PER, SPAN), F32),
            dma((CHUNKS, ranks)),
            dma((CHUNKS, ranks)),
            dma((CHUNKS, ranks * tensors)),
            dma((CHUNKS, ranks * tensors)),
            dma((ranks * 3,)),
            dma((ranks * 3,)),
            dma((contexts,)),
            dma((contexts,)),
            dma((2, CHUNKS)),
            dma((2, CHUNKS)),
            dma((CHUNKS, ranks)),
            dma((CHUNKS, ranks)),
            dma((ranks * 3,)),
            dma((ranks * 3,)),
            dma((4,)),
        ],
        compiler_params=pltpu.CompilerParams(
            collective_id=0, has_side_effects=True, vmem_limit_bytes=63 * 1024 * 1024
        ),
        name="mixer",
    )(head_inputs, input_map, output_map, step_sizes, grad_output, document[None, :], decay_rate[None, :])


def solution(mesh):
    placed = (
        P("context", "tensor"),
        P("tensor", "context"),
        P("tensor"),
        P("context", "tensor"),
        P("context", "tensor"),
        P("context"),
        P(("context", "tensor"), None),
    )
    return jax.shard_map(
        shards,
        mesh=mesh,
        in_specs=placed,
        out_specs=(
            P("context", "tensor"),
            P("tensor", "context"),
            P("context", "tensor"),
            P("context", "tensor"),
        ),
        check_vma=False,
    )
```

```python
import functools

import jax
import jax.numpy as jnp
from jax import lax
from jax.experimental import pallas as pl
from jax.experimental.pallas import tpu as pltpu
from jax.sharding import PartitionSpec as P

H = 128
P_SIZE = 64
N = 128
G = 8
SPAN = 128
PER = H // G
WIDE = PER * P_SIZE
LANES = 128
CHUNKS = 4
HC = PER // CHUNKS
CW = HC * P_SIZE
MESH = pl.DeviceIdType.MESH
BF = jnp.bfloat16
F32 = jnp.float32
NN = (((1,), (0,)), ((), ()))
NT = (((1,), (1,)), ((), ()))
TN = (((0,), (0,)), ((), ()))


def split(a):
    hi = a.astype(BF)
    return hi, (a - hi.astype(F32)).astype(BF)


def mm(a, b, dims=NN):
    return lax.dot_general(a, b, dims, preferred_element_type=F32)


def left2(a, b, dims=NN):
    hi, lo = split(a)
    return mm(hi, b, dims) + mm(lo, b, dims)


def right2(a, b, dims=NN):
    hi, lo = split(b)
    return mm(a, hi, dims) + mm(a, lo, dims)


def both3(a, b, dims=NN):
    ah, al = split(a)
    bh, bl = split(b)
    return mm(ah, bh, dims) + mm(ah, bl, dims) + mm(al, bh, dims)


def rows(k, size=SPAN):
    return pl.ds(k * size, size)


def mega_kernel(
    ranks, tensors, contexts, x, b, c, dt, dy, doc, rate_in, gi_o, gs_o, gb_o, gc_o,
    xg, dyg, bg, cg, dtg, docs, rates, s_in, a_in, s_out, a_out, fresh, message, decays, far, u, gi,
    tc, ltok, dttok, c_in, c_out, c_end, idcol, lhead, cross, neg, score, agree,
    dyy, xu, meets, gb, gc, gs,
    send_x, recv_x, send_dy, recv_dy, send_s, recv_s, send_doc, recv_doc,
    send_z, recv_z, send_o, recv_o, send_m, recv_m, local,
):
    planes = contexts // ranks
    last = planes - 1
    short = planes == 4
    lag = 2 if short else last
    context = lax.axis_index("context")
    tensor = lax.axis_index("tensor")
    rank = lax.rem(context, ranks)
    base = context - rank
    plane = lax.div(context, ranks)
    part = dy.shape[0]
    spot = pl.multiple_of(rank * SPAN, SPAN)
    spot_dy = pl.multiple_of((rank * tensors + tensor) * part, part)

    barrier = pltpu.get_barrier_semaphore()
    for d in range(1, contexts):
        pl.semaphore_signal(
            barrier, inc=1,
            device_id={"context": lax.rem(context + d, contexts), "tensor": tensor},
            device_id_type=MESH,
        )
    for dr in range(ranks):
        for du in range(1, tensors):
            pl.semaphore_signal(
                barrier, inc=1,
                device_id={
                    "context": base + lax.rem(rank + dr, ranks),
                    "tensor": lax.rem(tensor + du, tensors),
                },
                device_id_type=MESH,
            )
    pl.semaphore_wait(barrier, contexts - 1 + ranks * (tensors - 1))

    def remote(src, dst, send, recv, ctx, ten):
        return pltpu.make_async_remote_copy(
            src_ref=src, dst_ref=dst, send_sem=send, recv_sem=recv,
            device_id={"context": ctx, "tensor": ten}, device_id_type=MESH,
        )

    def doc_copy(d):
        to = lax.rem(context + d, contexts)
        return remote(doc, docs.at[context], send_doc.at[d], recv_doc.at[d], to, tensor)

    def small_copies(dr):
        to = lax.rem(rank + dr, ranks)
        at = pl.multiple_of(to * N, N)
        pairs = [
            (dt.at[pl.ds(pl.multiple_of(to * PER, PER), PER), :], dtg.at[rank]),
            (b.at[:, pl.ds(at, N)], bg.at[pl.ds(spot, SPAN), :]),
            (c.at[:, pl.ds(at, N)], cg.at[pl.ds(spot, SPAN), :]),
        ]
        if dr == 0:
            return [pltpu.make_async_copy(s, d, local.at[n]) for n, (s, d) in enumerate(pairs)]
        return [
            remote(s, d, send_s.at[dr * 3 + n], recv_s.at[dr * 3 + n], base + to, tensor)
            for n, (s, d) in enumerate(pairs)
        ]

    def chunk_copies(ch):
        copies = []
        for dr in list(range(1, ranks)) + [0]:
            to = lax.rem(rank + dr, ranks)
            src = x.at[:, pl.ds(pl.multiple_of(to * WIDE + ch * CW, CW), CW)]
            dst = xg.at[ch, pl.ds(spot, SPAN), :]
            if dr == 0:
                copies.append(pltpu.make_async_copy(src, dst, recv_x.at[ch, 0]))
            else:
                copies.append(
                    remote(src, dst, send_x.at[ch, dr], recv_x.at[ch, dr], base + to, tensor)
                )
            for du in range(tensors):
                tt = lax.rem(tensor + du, tensors)
                at = pl.multiple_of((tt * ranks + to) * WIDE + ch * CW, CW)
                src, dst = dy.at[:, pl.ds(at, CW)], dyg.at[ch, pl.ds(spot_dy, part), :]
                n = dr * tensors + du
                if n == 0:
                    copies.append(pltpu.make_async_copy(src, dst, recv_dy.at[ch, 0]))
                else:
                    copies.append(
                        remote(src, dst, send_dy.at[ch, n], recv_dy.at[ch, n], base + to, tt)
                    )
        return copies

    def wait_in(copy):
        if copy.is_remote:
            copy.wait_recv()
        else:
            copy.wait()

    own_doc = pltpu.make_async_copy(doc, docs.at[context], local.at[3])
    own_doc.start()
    for dr in list(range(1, ranks)) + [0]:
        for copy in small_copies(dr):
            copy.start()
    for d in range(1, contexts):
        doc_copy(d).start()
    for ch in range(CHUNKS):
        for copy in chunk_copies(ch):
            copy.start()

    @pl.when(plane == 0)
    def _():
        s_in[...] = jnp.zeros_like(s_in)

    @pl.when(plane == last)
    def _():
        a_in[...] = jnp.zeros_like(a_in)

    if short:

        @pl.when(plane <= 1)
        def _():
            far[0] = jnp.zeros_like(far[0])

        @pl.when(plane >= last - 1)
        def _():
            far[1] = jnp.zeros_like(far[1])

    score[...] = jnp.zeros_like(score)
    dyy[...] = jnp.zeros_like(dyy)
    xu[...] = jnp.zeros_like(xu)
    meets[...] = jnp.zeros_like(meets)
    gb[...] = jnp.zeros_like(gb)
    gc[...] = jnp.zeros_like(gc)

    row_i = lax.broadcasted_iota(jnp.int32, (SPAN, SPAN), 0)
    col_i = lax.broadcasted_iota(jnp.int32, (SPAN, SPAN), 1)
    ordered = row_i <= col_i
    up = ordered.astype(F32)
    pad = jnp.zeros((LANES - PER, SPAN), F32)

    heads = rate_in.shape[1]
    rate_wide = rate_in[...]
    if heads < LANES:
        rate_wide = jnp.concatenate([rate_wide, jnp.zeros((1, LANES - heads), F32)], axis=1)
    rates[...] = jnp.transpose(jnp.broadcast_to(rate_wide, (LANES, LANES)))
    rate = rates[pl.ds(pl.multiple_of(rank * PER, PER), PER), :]

    own_doc.wait()
    for d in range(1, contexts):
        doc_copy(d).wait_recv()
    for dr in list(range(1, ranks)) + [0]:
        for copy in small_copies(dr):
            wait_in(copy)
    before = docs[jnp.maximum(base - 1, 0)].astype(F32)[:, SPAN - 1 :]
    before = jnp.where(plane == 0, -1.0, before)
    after = docs[jnp.minimum(base + ranks, contexts - 1)].astype(F32)[:, :1]
    after = jnp.where(plane == last, -1.0, after)
    id_rows = [docs[base + k].astype(F32) for k in range(ranks)]
    for k in range(ranks):
        at = rows(k)
        id_row = id_rows[k]
        prev_id = id_rows[k - 1][:, SPAN - 1 :] if k else before
        next_id = id_rows[k + 1][:, :1] if k + 1 < ranks else after
        ids = jnp.transpose(jnp.broadcast_to(id_row, (SPAN, SPAN)))
        idcol[k] = ids
        steps = dtg[k]
        cum = lax.dot_general(
            -rate * steps, up, NN, precision=lax.Precision.HIGHEST, preferred_element_type=F32
        )
        cum_t = jnp.transpose(jnp.concatenate([cum, pad], axis=0))
        dt_t = jnp.transpose(jnp.concatenate([steps, pad], axis=0))
        ltok[at, :] = cum_t
        dttok[at, :] = dt_t
        for ch in range(CHUNKS):
            mine = slice(ch * HC, (ch + 1) * HC)
            both = jnp.concatenate([cum[mine], steps[mine]], axis=0)
            lhead[ch, k] = both
            tc[ch, at, :] = jnp.transpose(
                jnp.concatenate([both, jnp.zeros((LANES - 2 * HC, SPAN), F32)], axis=0)
            )
        rest = jnp.exp(cum_t[SPAN - 1 :, :] - cum_t)
        c_in[at, :] = jnp.where(ids == prev_id, jnp.exp(cum_t), 0.0)
        c_out[at, :] = jnp.where(ids == next_id, rest, 0.0)
        c_end[at, :] = jnp.where(ids == id_row[:, SPAN - 1 :], rest, 0.0) * dt_t
        neg[k] = jnp.where(ordered & (ids == id_row), 0.0, -1e30)
        cross[k] = mm(bg[at, :], cg[at, :], NT)

    lane_row = lax.broadcasted_iota(jnp.int32, (LANES, CW), 0)
    lane_col = lax.broadcasted_iota(jnp.int32, (LANES, CW), 1) // P_SIZE

    def spread_of(ch):
        return jnp.where(lane_row == lane_col + ch * HC, 1.0, 0.0).astype(BF)

    def summarise(ch):
        for copy in chunk_copies(ch):
            wait_in(copy)
        spread = spread_of(ch)
        for k in range(ranks):
            at = rows(k)
            xs = xg[ch, at, :].astype(F32) * left2(c_end[at, :], spread)
            in_e = left2(c_in[at, :], spread)
            dyc = dyg[ch, at, :].astype(F32) * in_e
            decays[ch, k] = in_e[SPAN - 1 :, :]
            fresh[ch, k] = right2(bg[at, :], xs, TN)
            message[ch, k] = right2(cg[at, :], dyc, TN)
        state = fresh[ch, 0]
        decay = decays[ch, 0]
        for k in range(1, ranks):
            state = decays[ch, k] * state + fresh[ch, k]
            decay = decays[ch, k] * decay
        s_out[ch] = state
        state = message[ch, ranks - 1]
        for k in range(ranks - 2, -1, -1):
            state = decays[ch, k] * state + message[ch, k]
        a_out[ch] = state
        decays[ch, ranks] = decay

    def s_copy(ch):
        return remote(
            s_out.at[ch], s_in.at[ch], send_z.at[0, ch], recv_z.at[0, ch],
            jnp.minimum(context + ranks, contexts - 1), tensor,
        )

    def a_copy(ch):
        return remote(
            a_out.at[ch], a_in.at[ch], send_z.at[1, ch], recv_z.at[1, ch],
            jnp.maximum(context - ranks, 0), tensor,
        )

    def s_far(ch):
        return remote(
            far.at[2, ch], far.at[0, ch], send_z.at[2, ch], recv_z.at[2, ch],
            jnp.minimum(context + ranks, contexts - 1), tensor,
        )

    def a_far(ch):
        return remote(
            far.at[3, ch], far.at[1, ch], send_z.at[3, ch], recv_z.at[3, ch],
            jnp.maximum(context - ranks, 0), tensor,
        )

    def pass_first(ch):
        @pl.when(plane < last)
        def _():
            s_copy(ch).start()

        @pl.when(plane > 0)
        def _():
            a_copy(ch).start()

    def pass_second(ch):
        @pl.when(plane > 0)
        def _():
            s_copy(ch).wait_recv()

        @pl.when((plane > 0) & (plane < last))
        def _():
            far[2, ch] = decays[ch, ranks] * s_in[ch]
            s_far(ch).start()

        @pl.when(plane < last)
        def _():
            a_copy(ch).wait_recv()

        @pl.when((plane > 0) & (plane < last))
        def _():
            far[3, ch] = decays[ch, ranks] * a_in[ch]
            a_far(ch).start()

    def pass_last(ch):
        @pl.when(plane > 1)
        def _():
            s_far(ch).wait_recv()

        @pl.when(plane < last - 1)
        def _():
            a_far(ch).wait_recv()

    def pass_state(ch):
        @pl.when(plane > 0)
        def _():
            s_copy(ch).wait_recv()

        @pl.when(plane < last)
        def _():
            s_out[ch] += decays[ch, ranks] * s_in[ch]
            s_copy(ch).start()

    def pass_adjoint(ch):
        @pl.when(plane < last)
        def _():
            a_copy(ch).wait_recv()

        @pl.when(plane > 0)
        def _():
            a_out[ch] += decays[ch, ranks] * a_in[ch]
            a_copy(ch).start()

    def inside(ch):
        def block(k, carry):
            at = pl.ds(pl.multiple_of(k * SPAN, SPAN), SPAN)
            cross_t = cross[k]
            hide = neg[k]
            total = score[k]
            x_k, dy_k, cols, heads = xg[ch, at, :], dyg[ch, at, :], tc[ch, at, :], lhead[ch, k]
            agrees = []
            for h in range(HC):
                cut = slice(h * P_SIZE, (h + 1) * P_SIZE)
                x_h, dy_h = x_k[:, cut], dy_k[:, cut]
                w = jnp.exp((heads[h : h + 1, :] - cols[:, h : h + 1]) + hide)
                u[ch, at, cut] = left2(w * cross_t, dy_h)
                q = w * mm(x_h, dy_h, NT) * cols[:, HC + h : HC + h + 1]
                total = total + q
                agrees.append(jnp.sum(q * cross_t, axis=0, keepdims=True))
            score[k] = total
            agree[ch, k] = jnp.concatenate(agrees, axis=0)
            return carry

        lax.fori_loop(0, ranks, block, 0)

    def gi_pair(ch, to):
        return (
            gi.at[ch, pl.ds(to * SPAN, SPAN), :],
            gi_o.at[:, pl.ds(pl.multiple_of(rank * WIDE + ch * CW, CW), CW)],
        )

    def gi_local(ch, to):
        return pltpu.make_async_copy(*gi_pair(ch, to), recv_o.at[ch, rank])

    def gi_remote(ch, to):
        return remote(
            *gi_pair(ch, to), send_o.at[ch, to], recv_o.at[ch, rank], base + to, tensor
        )

    def gi_start(ch, to):
        @pl.when(rank == to)
        def _():
            gi_local(ch, to).start()

        @pl.when(rank != to)
        def _():
            gi_remote(ch, to).start()

    def gi_wait(ch, other):
        @pl.when(rank == other)
        def _():
            gi_local(ch, other).wait()

        @pl.when(rank != other)
        def _():
            remote(
                *gi_pair(ch, other), send_o.at[ch, other], recv_o.at[ch, other], base + other, tensor
            ).wait()

    def finish(ch):
        spread = spread_of(ch)
        states = [s_in[ch] + far[0, ch] if short else s_in[ch]]
        for k in range(ranks):
            states.append(decays[ch, k] * states[k] + fresh[ch, k])
        adj = a_in[ch] + far[1, ch] if short else a_in[ch]
        for k in range(ranks - 1, -1, -1):
            at = rows(k)
            in_e = left2(c_in[at, :], spread)
            out_e = left2(c_out[at, :], spread)
            dt_e = left2(dttok[at, :], spread)
            state = states[k]
            x_f = xg[ch, at, :].astype(F32)
            dyc = dyg[ch, at, :].astype(F32) * in_e
            total_u = u[ch, at, :] + right2(bg[at, :], adj) * out_e
            gi[ch, at, :] = (total_u * dt_e).astype(BF)
            gi_start(ch, k)
            gc[at, :] += both3(dyc, state, NT)
            gb[at, :] += both3(x_f * out_e * dt_e, adj, NT)
            dyy[at, :] += left2(dyc * right2(cg[at, :], state), spread, NT)
            xu[at, :] += left2(x_f * total_u, spread, NT)
            meet = jnp.sum(states[k + 1] * adj, axis=0, keepdims=True)
            meets[k] += left2(jnp.broadcast_to(meet, (8, CW)), spread, NT)
            adj = decays[ch, k] * adj + message[ch, k]
    def step(it, carry):
        @pl.when(it < CHUNKS)
        def _():
            summarise(it)

        if short:

            @pl.when(it < CHUNKS)
            def _():
                pass_first(it)

            @pl.when((it >= 1) & (it <= CHUNKS))
            def _():
                pass_second(it - 1)

        else:
            ahead = it - plane

            @pl.when((ahead >= 0) & (ahead < CHUNKS))
            def _():
                pass_state(ahead)

            behind = it - (last - plane)

            @pl.when((behind >= 0) & (behind < CHUNKS))
            def _():
                pass_adjoint(behind)

        @pl.when(it < CHUNKS)
        def _():
            inside(it)

        @pl.when(it >= lag)
        def _():
            if short:
                pass_last(it - lag)
            finish(it - lag)

        return carry

    lax.fori_loop(0, CHUNKS + lag, step, 0)

    def map_copies(to, source):
        there = pl.ds(to * SPAN, SPAN)
        at = pl.ds(pl.multiple_of(rank * N, N), N)
        pairs = [
            (gb.at[there, :], gb_o.at[:, at]),
            (gc.at[there, :], gc_o.at[:, at]),
            (gs.at[to], gs_o.at[pl.ds(pl.multiple_of(rank * PER, PER), PER), :]),
        ]
        own = [pltpu.make_async_copy(s, d, local.at[n]) for n, (s, d) in enumerate(pairs)]
        away = [
            remote(
                s, d, send_m.at[to * 3 + n], recv_m.at[source * 3 + n], base + to, tensor
            )
            for n, (s, d) in enumerate(pairs)
        ]
        return own, away

    def map_do(to, source, act):
        own, away = map_copies(to, source)

        @pl.when(rank == to)
        def _():
            for copy in own:
                act(copy)

        @pl.when(rank != to)
        def _():
            for copy in away:
                act(copy)

    rate_row = jnp.transpose(
        jnp.concatenate([rates[pl.ds(pl.multiple_of(rank * PER, PER), PER), :], pad], axis=0)
    )
    for k in range(ranks):
        at = rows(k)
        id_row = id_rows[k]
        next_id = id_rows[k + 1][:, :1] if k + 1 < ranks else after
        ids = idcol[k]
        gb[at, :] += left2(score[k], cg[at, :])
        gc[at, :] += left2(score[k], bg[at, :], TN)
        agree_k = jnp.concatenate([agree[ch, k] for ch in range(CHUNKS)] + [pad], axis=0)
        slope = jnp.transpose(agree_k) + dyy[at, :] - dttok[at, :] * xu[at, :]
        same = jnp.where((ids == id_row) & ordered, 1.0, 0.0).astype(BF)
        tails = right2(same, slope) + jnp.where(ids == next_id, meets[k][:1], 0.0)
        gs[k] = jnp.transpose(xu[at, :] - rate_row * tails)[:PER, :]
        map_do(k, rank, lambda copy: copy.start())

    order = list(range(1, ranks)) + [0]
    for d in range(1, contexts):
        doc_copy(d).wait_send()
    for dr in order[:-1]:
        for copy in small_copies(dr):
            copy.wait_send()
    for ch in range(CHUNKS):
        for copy in chunk_copies(ch):
            if copy.is_remote:
                copy.wait_send()
        for other in range(ranks):
            gi_wait(ch, other)

        @pl.when(plane < last)
        def _():
            s_copy(ch).wait_send()

        @pl.when(plane > 0)
        def _():
            a_copy(ch).wait_send()

        if short:

            @pl.when((plane > 0) & (plane < last))
            def _():
                s_far(ch).wait_send()
                a_far(ch).wait_send()

    for other in range(ranks):
        map_do(other, other, lambda copy: copy.wait())


def shards(head_inputs, step_sizes, decay_rate, input_map, output_map, document, grad_output):
    heads_here = decay_rate.shape[0]
    ranks = heads_here // PER
    contexts = lax.axis_size("context")
    tensors = lax.axis_size("tensor")
    tokens = ranks * SPAN
    hbm = pl.BlockSpec(memory_space=pltpu.HBM)
    vmem = pl.BlockSpec(memory_space=pltpu.VMEM)
    shape = jax.ShapeDtypeStruct
    mem = pltpu.VMEM
    dma = pltpu.SemaphoreType.DMA
    return pl.pallas_call(
        functools.partial(mega_kernel, ranks, tensors, contexts),
        out_shape=(
            shape((SPAN, ranks * WIDE), BF),
            shape((heads_here, SPAN), F32),
            shape((SPAN, ranks * N), F32),
            shape((SPAN, ranks * N), F32),
        ),
        in_specs=[hbm] * 5 + [vmem] * 2,
        out_specs=(hbm,) * 4,
        scratch_shapes=[
            mem((CHUNKS, tokens, CW), BF),
            mem((CHUNKS, tokens, CW), BF),
            mem((tokens, N), BF),
            mem((tokens, N), BF),
            mem((ranks, PER, SPAN), F32),
            mem((contexts, 1, SPAN), jnp.int32),
            mem((LANES, LANES), F32),
            mem((CHUNKS, N, CW), F32),
            mem((CHUNKS, N, CW), F32),
            mem((CHUNKS, N, CW), F32),
            mem((CHUNKS, N, CW), F32),
            mem((CHUNKS, ranks, N, CW), F32),
            mem((CHUNKS, ranks, N, CW), F32),
            mem((CHUNKS, ranks + 1, 1, CW), F32),
            mem((4, CHUNKS, N, CW), F32),
            mem((CHUNKS, tokens, CW), F32),
            mem((CHUNKS, tokens, CW), BF),
            mem((CHUNKS, tokens, LANES), F32),
            mem((tokens, LANES), F32),
            mem((tokens, LANES), F32),
            mem((tokens, LANES), F32),
            mem((tokens, LANES), F32),
            mem((tokens, LANES), F32),
            mem((ranks, SPAN, SPAN), F32),
            mem((CHUNKS, ranks, 2 * HC, SPAN), F32),
            mem((ranks, SPAN, SPAN), F32),
            mem((ranks, SPAN, SPAN), F32),
            mem((ranks, SPAN, SPAN), F32),
            mem((CHUNKS, ranks, HC, SPAN), F32),
            mem((tokens, LANES), F32),
            mem((tokens, LANES), F32),
            mem((ranks, 8, LANES), F32),
            mem((tokens, N), F32),
            mem((tokens, N), F32),
            mem((ranks, PER, SPAN), F32),
            dma((CHUNKS, ranks)),
            dma((CHUNKS, ranks)),
            dma((CHUNKS, ranks * tensors)),
            dma((CHUNKS, ranks * tensors)),
            dma((ranks * 3,)),
            dma((ranks * 3,)),
            dma((contexts,)),
            dma((contexts,)),
            dma((4, CHUNKS)),
            dma((4, CHUNKS)),
            dma((CHUNKS, ranks)),
            dma((CHUNKS, ranks)),
            dma((ranks * 3,)),
            dma((ranks * 3,)),
            dma((4,)),
        ],
        compiler_params=pltpu.CompilerParams(
            collective_id=0, has_side_effects=True, vmem_limit_bytes=63 * 1024 * 1024
        ),
        name="mixer",
    )(head_inputs, input_map, output_map, step_sizes, grad_output, document[None, :], decay_rate[None, :])


def solution(mesh):
    placed = (
        P("context", "tensor"),
        P("tensor", "context"),
        P("tensor"),
        P("context", "tensor"),
        P("context", "tensor"),
        P("context"),
        P(("context", "tensor"), None),
    )
    return jax.shard_map(
        shards,
        mesh=mesh,
        in_specs=placed,
        out_specs=(
            P("context", "tensor"),
            P("tensor", "context"),
            P("context", "tensor"),
            P("context", "tensor"),
        ),
        check_vma=False,
    )
```
